32 devices in a mesh: seq: 32 (over z, y, x, core).
Axes of the slice: x: 2, y: 2, z: 4, core: 2. Of those that a mesh axis runs over, the one named last changes fastest.
Arguments:
- tokens: bfloat16 [32768, 1024], P('seq'), may hold values from -16 to 16
- w_query: bfloat16 [1024, 1024], replicated, may hold values from -0.1875 to 0.1875
- w_key: bfloat16 [1024, 1024], replicated, may hold values from -0.1875 to 0.1875
- w_value: bfloat16 [1024, 1024], replicated, may hold values from -0.1875 to 0.1875
- w_out: bfloat16 [1024, 1024], replicated, may hold values from -0.1875 to 0.1875
- rand_blocks: int32 [512, 3], P('seq'), may hold values from 0 to 511, as said below
- global_pos: int32 [128], replicated, may hold values from 0 to 32767, as said below
Outputs:
- mixed: bfloat16 [32768, 1024], P('seq')
The draws below stay inside these ranges and needn't reach their ends.
Inputs may be any that keep to these rules, and one draw needn't show every extreme that they name: `rand_blocks`: the entries of a row differ, and none is the row's block or a block next to it. All entries lie on the row's own device (blocks of 16 per device, contiguous), except that for each device and each offset o of -3 to -1 and 1 to 3 for which a device o away exists, exactly one row of the device has its last entry on the device o away. `global_pos`: distinct and increasing.
All inputs are finite; a program needn't handle non-finite values.
Results may differ from the reference program's by a relative error of at most 0.003.
The reference program's roundings to bfloat16 on the way count: a program that leaves them out, or rounds other values in their place, can miss the bound.
Values may be sent and summed in bfloat16 or wider, within the bound.
A program may use at most 192 MiB of HBM per device.

```python
import math
import jax
import jax.numpy as jnp
from jax import lax

D = 1024
HEADS = 16
HD = 64
BLK = 64
RAND = 3
NG = 128
FAR = 3
TOK_DEV = 1024
NBLOCKS = 512
TOKENS = 32768
N_SEQ = 32


def draw_tokens(key, part):
    first_key = jax.random.fold_in(key, 0)
    values = jnp.clip(jax.random.normal(first_key, (TOKENS, D), jnp.float32), -6.0, 6.0)
    return values.astype(jnp.bfloat16)


def draw_rand_blocks(key, part):
    block_count = TOK_DEV // BLK
    seq_count = NBLOCKS // block_count
    first_key, second_key, third_key = jax.random.split(key, 3)
    local_index = jnp.arange(NBLOCKS, dtype=jnp.int32) % block_count
    candidates = jnp.arange(block_count, dtype=jnp.int32)
    scores = jax.random.randint(first_key, (NBLOCKS, block_count), 0, 65536) * block_count + candidates[None, :]
    allowed = jnp.abs(candidates[None, :] - local_index[:, None]) > 1
    scores = jnp.where(allowed, scores, -1)
    top_values, chosen = lax.top_k(scores, RAND)
    device_of_row = jnp.arange(NBLOCKS, dtype=jnp.int32) // block_count
    chosen = chosen.astype(jnp.int32) + device_of_row[:, None] * block_count
    device_keys = jax.random.split(second_key, seq_count)
    chosen_rows = jax.vmap(lambda item_key: jax.random.permutation(item_key, block_count))(device_keys)[:, :2 * FAR]
    chosen_rows = chosen_rows.astype(jnp.int32)
    offsets = jnp.concatenate([jnp.arange(-FAR, 0), jnp.arange(1, FAR + 1)]).astype(jnp.int32)
    device_ids = jnp.arange(seq_count, dtype=jnp.int32)[:, None]
    target = device_ids + offsets[None, :]
    in_range = (target >= 0) & (target < seq_count)
    far_local = jax.random.randint(third_key, (seq_count, 2 * FAR), 1, block_count - 1).astype(jnp.int32)
    row_ids = (device_ids * block_count + chosen_rows).reshape(-1)
    old_last = chosen[row_ids, RAND - 1].reshape(seq_count, 2 * FAR)
    new_last = jnp.where(in_range, target * block_count + far_local, old_last).reshape(-1)
    last_column = chosen[:, RAND - 1].at[row_ids].set(new_last)
    return chosen.at[:, RAND - 1].set(last_column).astype(jnp.int32)


def draw_global_pos(key, part):
    shuffled = jax.random.permutation(key, TOKENS)[:NG]
    return jnp.sort(shuffled).astype(jnp.int32)


def bell_draw(rng, dims, deviation, limit, kind=jnp.bfloat16):
    array = deviation * jax.random.normal(rng, dims, jnp.float32)
    return jnp.clip(array, min=-limit, max=limit).astype(kind)


def setup_inputs(seed: int = 0) -> dict:
    key_of = jax.random.split(jax.random.key(seed), 8)
    tokens = draw_tokens(jax.random.fold_in(key_of[7], 71), 0)
    w_query = bell_draw(key_of[1], (D, D), D ** -0.5, 0.1875)
    w_key = bell_draw(key_of[2], (D, D), D ** -0.5, 0.1875)
    w_value = bell_draw(key_of[3], (D, D), D ** -0.5, 0.1875)
    w_out = bell_draw(key_of[4], (D, D), D ** -0.5, 0.1875)
    rand_blocks = draw_rand_blocks(jax.random.fold_in(key_of[7], 71), 0)
    global_pos = draw_global_pos(jax.random.fold_in(key_of[7], 71), 0)
    return dict(tokens=tokens, w_query=w_query, w_key=w_key, w_value=w_value, w_out=w_out, rand_blocks=rand_blocks, global_pos=global_pos)


def reference(tokens, w_query, w_key, w_value, w_out, rand_blocks, global_pos):
    queries = jnp.dot(tokens, w_query, preferred_element_type=jnp.float32).astype(jnp.bfloat16)
    keys = jnp.dot(tokens, w_key, preferred_element_type=jnp.float32).astype(jnp.bfloat16)
    values = jnp.dot(tokens, w_value, preferred_element_type=jnp.float32).astype(jnp.bfloat16)
    block_count = tokens.shape[0] // BLK
    query_blocks = queries.reshape(block_count, BLK, HEADS, HD)
    key_blocks = keys.reshape(block_count, BLK, HEADS, HD)
    value_blocks = values.reshape(block_count, BLK, HEADS, HD)
    global_keys = keys[global_pos].reshape(NG, HEADS, HD).astype(jnp.float32)
    global_values = values[global_pos].reshape(NG, HEADS, HD).astype(jnp.float32)
    score_scale = 1.0 / math.sqrt(HD)
    group_size = math.gcd(block_count, max(1, 512 // BLK))

    def attend_group(start):
        block_ids = start + jnp.arange(group_size, dtype=jnp.int32)
        window = jnp.stack([block_ids - 1, block_ids, block_ids + 1], axis=1)
        window_ok = (window >= 0) & (window < block_count)
        chosen = lax.dynamic_slice_in_dim(rand_blocks, start, group_size, 0).astype(jnp.int32)
        index_set = jnp.concatenate([jnp.clip(window, 0, block_count - 1), chosen], axis=1)
        valid_set = jnp.concatenate([window_ok, jnp.ones((group_size, RAND), bool)], axis=1)
        key_heads = key_blocks[index_set].reshape(group_size, -1, HEADS, HD).astype(jnp.float32)
        value_heads = value_blocks[index_set].reshape(group_size, -1, HEADS, HD).astype(jnp.float32)
        key_valid = jnp.repeat(valid_set, BLK, axis=1)
        query_group = lax.dynamic_slice_in_dim(query_blocks, start, group_size, 0).astype(jnp.float32)
        local_scores = jnp.einsum('gqhd,gkhd->ghqk', query_group, key_heads) * score_scale
        local_scores = jnp.where(key_valid[:, None, None, :], local_scores, -1e+30)
        global_scores = jnp.einsum('gqhd,khd->ghqk', query_group, global_keys) * score_scale
        all_scores = jnp.concatenate([local_scores, global_scores], axis=-1)
        top_score = lax.optimization_barrier(jnp.max(all_scores, axis=-1, keepdims=True))
        exps = jnp.exp(all_scores - top_score)
        weights = lax.optimization_barrier((exps / lax.optimization_barrier(jnp.sum(exps, axis=-1, keepdims=True))).astype(jnp.bfloat16))
        weights = weights.astype(jnp.float32)
        split_at = key_heads.shape[1]
        result = jnp.einsum('ghqk,gkhd->gqhd', weights[..., :split_at], value_heads)
        result = result + jnp.einsum('ghqk,khd->gqhd', weights[..., split_at:], global_values)
        return result.astype(jnp.bfloat16)
    starts = jnp.arange(0, block_count, group_size, dtype=jnp.int32)
    sparse = lax.map(attend_group, starts).reshape(-1, D)
    global_queries = queries[global_pos].reshape(NG, HEADS, HD).astype(jnp.float32)
    key_shards = keys.reshape(N_SEQ, -1, HEADS, HD)
    value_shards = values.reshape(N_SEQ, -1, HEADS, HD)

    def shard_sums(shard):
        shard_keys = key_shards[shard].astype(jnp.float32)
        shard_values = value_shards[shard].astype(jnp.float32)
        gscore = jnp.einsum('qhd,khd->hqk', global_queries, shard_keys) * score_scale
        speak = lax.optimization_barrier(jnp.max(gscore, axis=-1))
        gexp = jnp.exp(gscore - speak[:, :, None])
        stotal = lax.optimization_barrier(jnp.sum(gexp, axis=-1))
        rounded = lax.optimization_barrier(gexp.astype(jnp.bfloat16)).astype(jnp.float32)
        snum = jnp.einsum('hqk,khd->qhd', rounded, shard_values)
        return (speak, stotal, snum)
    shard_ids = jnp.arange(N_SEQ, dtype=jnp.int32)
    peaks, totals, numerators = lax.map(shard_sums, shard_ids)
    peak_score = lax.optimization_barrier(jnp.max(peaks, axis=0))
    factors = jnp.exp(peaks - peak_score[None])
    gtotal = lax.optimization_barrier(jnp.sum(totals * factors, axis=0))
    gnum = lax.optimization_barrier(jnp.sum(numerators * jnp.transpose(factors, (0, 2, 1))[:, :, :, None], axis=0))
    gout = (gnum / jnp.transpose(gtotal)[:, :, None]).reshape(NG, D).astype(jnp.bfloat16)
    attended = sparse.at[global_pos].set(gout)
    return jnp.dot(attended, w_out, preferred_element_type=jnp.float32).astype(jnp.bfloat16)
```

```python
import functools
import math

import jax
import jax.numpy as jnp
from jax import lax
from jax.experimental import pallas as pl
from jax.experimental.pallas import tpu as pltpu
from jax.sharding import PartitionSpec as P

HEADS = 16
HD = 64
BLK = 64
RAND = 3
NG = 128
FAR = 3
OFFSETS = tuple(range(-FAR, 0)) + tuple(range(1, FAR + 1))
NFAR = len(OFFSETS)
GH = 4
GL = GH * HD
EXP_SCALE = math.log2(math.e) / math.sqrt(HD)
SCORE_SCALE = 1.0 / math.sqrt(HD)
MESH = pl.DeviceIdType.MESH
BF = jnp.bfloat16
F32 = jnp.float32


def mega(
    n,
    tok_hbm, wq_hbm, wk_hbm, wv_hbm, wo_hbm, req_ref, gcol_ref, grow_ref, idx_ref,
    out_ref,
    text, wq, wk, wv, wo, q, k, v, gq, sp, gf, sel, far,
    reqin, rs_out, rs_in, ag, cn_out, cn_in, cs_out, cs_in, ag2,
    load_sem, req_s, req_r, edge_s, edge_r,
    rs_s, rs_r, ag_s, ag_r, cn_s, cn_r, cs_s, cs_r, ag2_s, ag2_r,
):
    tok_dev, width = tok_hbm.shape
    nblk = tok_dev // BLK
    me = lax.axis_index("seq")
    _, rb, cb = ag.shape
    ncg = width // cb
    hpb = cb // HD
    groups = width // GL
    right0 = BLK + tok_dev
    far0 = right0 + BLK
    glob0 = far0 + NFAR * BLK

    own = text.at[pl.ds(BLK, tok_dev)]
    loads = [
        pltpu.make_async_copy(src, dst, load_sem.at[i])
        for i, (src, dst) in enumerate(
            ((tok_hbm, own), (wq_hbm, wq), (wk_hbm, wk), (wv_hbm, wv), (wo_hbm, wo))
        )
    ]
    for cp in loads:
        cp.start()

    text[0:BLK] = jnp.zeros((BLK, width), BF)
    text[right0:glob0] = jnp.zeros((glob0 - right0, width), BF)
    reqin[...] = jnp.zeros(reqin.shape, jnp.int32)

    barrier = pltpu.get_barrier_semaphore()

    def greet(o, c):
        pl.semaphore_signal(
            barrier, inc=1, device_id=(lax.rem(me + o, n),), device_id_type=MESH
        )
        return c

    lax.fori_loop(1, n, greet, 0)
    pl.semaphore_wait(barrier, n - 1)

    def to_all(src, dst, s_sem, r_sem):
        def one(o, c):
            peer = lax.rem(me + o, n)
            pltpu.make_async_remote_copy(
                src_ref=src(peer), dst_ref=dst.at[me], send_sem=s_sem, recv_sem=r_sem,
                device_id=(peer,), device_id_type=MESH,
            ).start()
            return c

        lax.fori_loop(1, n, one, 0)

    def wait_bytes(buf, sem):
        part = buf.at[pl.ds(0, n - 1)]
        pltpu.make_async_copy(part, part, sem).wait()

    def req_copy(i):
        return pltpu.make_async_remote_copy(
            src_ref=req_ref.at[i], dst_ref=reqin.at[i], send_sem=req_s.at[i],
            recv_sem=req_r.at[i], device_id=(me + OFFSETS[i],), device_id_type=MESH,
        )

    def far_copy(i):
        return pltpu.make_async_remote_copy(
            src_ref=far.at[pl.ds(i * BLK, BLK)],
            dst_ref=text.at[pl.ds(far0 + i * BLK, BLK)],
            send_sem=edge_s.at[2 + i], recv_sem=edge_r.at[2 + i],
            device_id=(me - OFFSETS[i],), device_id_type=MESH,
        )

    def halo_copy(side):
        if side == 0:
            src, dst, dev = (BLK, right0, me - 1)
        else:
            src, dst, dev = (right0 - BLK, 0, me + 1)
        return pltpu.make_async_remote_copy(
            src_ref=text.at[pl.ds(src, BLK)], dst_ref=text.at[pl.ds(dst, BLK)],
            send_sem=edge_s.at[side], recv_sem=edge_r.at[side],
            device_id=(dev,), device_id_type=MESH,
        )

    def exists(o):
        return me + o >= 0 if o < 0 else me + o < n

    for i, o in enumerate(OFFSETS):
        @pl.when(exists(o))
        def _():
            req_copy(i).start()

    loads[0].wait()
    for side, o in ((0, -1), (1, 1)):
        @pl.when(exists(o))
        def _():
            halo_copy(side).start()

    def project(src, s0, rows, w, dst, d0, step):
        def one(c, carry):
            a = pl.multiple_of(s0 + c * step, BLK)
            b = pl.multiple_of(d0 + c * step, BLK)
            val = jnp.dot(
                src[pl.ds(a, step)], w[...], preferred_element_type=F32
            ).astype(dst.dtype)
            if len(dst.shape) == 3:
                dst[pl.ds(d0 // BLK + c * (step // BLK), step // BLK)] = val.reshape(
                    step // BLK, BLK, width
                )
            else:
                dst[pl.ds(b, step)] = val
            return carry

        lax.fori_loop(0, rows // step, one, 0)

    hit = gcol_ref[...] == me * tok_dev + lax.broadcasted_iota(jnp.int32, (NG, tok_dev), 1)
    sel[0:NG] = jnp.where(hit, 1.0, 0.0).astype(BF)
    project(sel, 0, NG, own, gf, 0, NG)
    for d in range(n):
        r, c = (d // ncg) * rb, (d % ncg) * cb
        rs_out[d] = gf[r:r + rb, c:c + cb].astype(BF)
    to_all(lambda p: rs_out.at[p], rs_in, rs_s, rs_r)

    for i, o in enumerate(OFFSETS):
        @pl.when(exists(-o))
        def _():
            req_copy(i).wait_recv()
    col = lax.broadcasted_iota(jnp.int32, (BLK, tok_dev), 1)
    row = lax.broadcasted_iota(jnp.int32, (BLK, tok_dev), 0)
    for i in range(NFAR):
        want = reqin[i, 0:1, 0:1] * BLK
        sel[i * BLK:(i + 1) * BLK] = jnp.where(col == want + row, 1.0, 0.0).astype(BF)
    project(sel, 0, NFAR * BLK, own, far, 0, 2 * BLK)
    for i, o in enumerate(OFFSETS):
        @pl.when(exists(-o))
        def _():
            far_copy(i).start()

    loads[1].wait()
    project(text, BLK, tok_dev, wq, q, 0, 256)

    rs_in[me] = rs_out[me]
    wait_bytes(rs_in, rs_r)
    ag[me] = jnp.sum(rs_in[...].astype(F32), axis=0).astype(BF)
    to_all(lambda p: ag.at[me], ag, ag_s, ag_r)

    loads[2].wait()
    project(text, BLK, tok_dev, wk, k, BLK, 256)
    loads[3].wait()
    project(text, BLK, tok_dev, wv, v, BLK, 256)

    wait_bytes(ag, ag_r)
    for d in range(n):
        r, c = (d // ncg) * rb, (d % ncg) * cb
        gf[r:r + rb, c:c + cb] = ag[d].astype(F32)
    text[glob0:glob0 + NG] = gf[...].astype(BF)
    project(text, glob0, NG, wq, gq, 0, NG)

    lane = lax.broadcasted_iota(jnp.int32, (1, GL), 1) // HD
    masks = [jnp.where(lane == h, 1.0, 0.0).astype(BF) for h in range(GH)]
    lane_f = lax.broadcasted_iota(jnp.int32, (1, 128), 1)

    def stacked(x):
        return jnp.concatenate([x * m for m in masks], axis=0)

    def unstacked(x, rows):
        y = x[0:rows]
        for h in range(1, GH):
            y = jnp.where(lane == h, x[h * rows:(h + 1) * rows], y)
        return y

    NT = (((1,), (1,)), ((), ()))
    for g in range(groups):
        ls = slice(g * GL, (g + 1) * GL)
        s = lax.dot_general(
            stacked(gq[:, ls]), k[1:1 + nblk, :, ls].reshape(tok_dev, GL), NT, preferred_element_type=F32
        )
        m = jnp.max(s, axis=-1, keepdims=True)
        e = jnp.exp2((s - m) * EXP_SCALE)
        t = jnp.sum(e, axis=-1, keepdims=True)
        num = unstacked(
            jnp.dot(e.astype(BF), v[1:1 + nblk, :, ls].reshape(tok_dev, GL), preferred_element_type=F32), NG
        )
        m = m * SCORE_SCALE
        for part in range(GL // cb):
            stat = jnp.zeros((NG, 128), F32)
            for j in range(hpb):
                h = part * hpb + j
                stat = jnp.where(lane_f == j, m[h * NG:(h + 1) * NG], stat)
                stat = jnp.where(lane_f == hpb + j, t[h * NG:(h + 1) * NG], stat)
            cg = g * (GL // cb) + part
            for rg in range(NG // rb):
                d = rg * ncg + cg
                cn_out[d] = num[rg * rb:(rg + 1) * rb, part * cb:(part + 1) * cb].astype(BF)
                cs_out[d] = stat[rg * rb:(rg + 1) * rb]
    to_all(lambda p: cs_out.at[p], cs_in, cs_s, cs_r)
    to_all(lambda p: cn_out.at[p], cn_in, cn_s, cn_r)

    for side, o in ((0, 1), (1, -1)):
        @pl.when(exists(o))
        def _():
            halo_copy(side).wait_recv()
    for i, o in enumerate(OFFSETS):
        @pl.when(exists(o))
        def _():
            far_copy(i).wait_recv()
    for w, dst in ((wk, k), (wv, v)):
        project(text, 0, BLK, w, dst, 0, BLK)
        project(text, right0, glob0 + NG - right0, w, dst, right0, 192)

    keys_all = (3 + RAND) * BLK + NG
    key_col = lax.broadcasted_iota(jnp.int32, (1, keys_all), 1)

    def attend(b, carry):
        lead = jnp.where((me == 0) & (b == 0), BLK, 0)
        tail = jnp.where((me == n - 1) & (b == nblk - 1), 2 * BLK, 3 * BLK)
        bad = (key_col < lead) | ((key_col >= tail) & (key_col < 3 * BLK))
        bias = jnp.where(bad, -1e30, 0.0)
        at = pl.multiple_of(b * BLK, BLK)
        picks = [idx_ref[b * RAND + r] for r in range(RAND)]

        def rows(ref, ls):
            return jnp.concatenate(
                [ref[pl.ds(b, 3), :, ls].reshape(3 * BLK, GL)]
                + [ref[i, :, ls] for i in picks]
                + [ref[glob0 // BLK:, :, ls].reshape(NG, GL)],
                axis=0,
            )

        for g in range(groups):
            ls = slice(g * GL, (g + 1) * GL)
            s = lax.dot_general(
                stacked(q[pl.ds(at, BLK), ls]), rows(k, ls), NT, preferred_element_type=F32
            )
            s = s + bias
            m = jnp.max(s, axis=-1, keepdims=True)
            e = jnp.exp2((s - m) * EXP_SCALE)
            inv = 1.0 / jnp.sum(e, axis=-1, keepdims=True)
            o = jnp.dot((e * inv).astype(BF), rows(v, ls), preferred_element_type=F32)
            sp[pl.ds(at, BLK), ls] = unstacked(o, BLK).astype(BF)
        return carry

    lax.fori_loop(0, nblk // 2, attend, 0)

    cs_in[me] = cs_out[me]
    cn_in[me] = cn_out[me]
    wait_bytes(cs_in, cs_r)
    wait_bytes(cn_in, cn_r)
    peak = jnp.max(cs_in[...], axis=0)
    lane_c = lax.broadcasted_iota(jnp.int32, (1, cb), 1) // HD

    def spread(x, first):
        y = jnp.broadcast_to(x[:, first:first + 1], (rb, cb))
        for j in range(1, hpb):
            y = jnp.where(lane_c == j, x[:, first + j:first + j + 1], y)
        return y

    def merge(s, c):
        num, den = c
        stat = cs_in[s]
        fac = spread(jnp.exp(stat - peak), 0)
        return num + cn_in[s].astype(F32) * fac, den + spread(stat, hpb) * fac

    zero = jnp.zeros((rb, cb), F32)
    num, den = lax.fori_loop(0, n, merge, (zero, zero))
    ag2[me] = (num / den).astype(BF)
    to_all(lambda p: ag2.at[me], ag2, ag2_s, ag2_r)

    lax.fori_loop(nblk // 2, nblk, attend, 0)

    wait_bytes(ag2, ag2_r)
    for d in range(n):
        r, c = (d // ncg) * rb, (d % ncg) * cb
        gf[r:r + rb, c:c + cb] = ag2[d].astype(F32)
    gq[...] = gf[...].astype(BF)
    loads[4].wait()
    step = 256

    def finish(c, carry):
        at = pl.multiple_of(c * step, step)
        pos = me * tok_dev + at + lax.broadcasted_iota(jnp.int32, (step, NG), 0)
        one = jnp.where(pos == grow_ref[...], 1.0, 0.0)
        is_g = jnp.max(one, axis=-1, keepdims=True) > 0.5
        put = jnp.dot(one.astype(BF), gq[...], preferred_element_type=F32)
        att = jnp.where(is_g, put, sp[pl.ds(at, step)].astype(F32)).astype(BF)
        out_ref[pl.ds(at, step)] = jnp.dot(
            att, wo[...], preferred_element_type=F32
        ).astype(BF)
        return carry

    lax.fori_loop(0, tok_dev // step, finish, 0)

    for i, o in enumerate(OFFSETS):
        @pl.when(exists(o))
        def _():
            req_copy(i).wait_send()

        @pl.when(exists(-o))
        def _():
            far_copy(i).wait_send()
    for side, o in ((0, -1), (1, 1)):
        @pl.when(exists(o))
        def _():
            halo_copy(side).wait_send()
    for buf, sem in ((rs_out, rs_s), (ag, ag_s), (cn_out, cn_s), (cs_out, cs_s), (ag2, ag2_s)):
        wait_bytes(buf, sem)


def body(n, tokens, w_query, w_key, w_value, w_out, rand_blocks, global_pos):
    tok_dev, width = tokens.shape
    nblk = tok_dev // BLK
    me = lax.axis_index("seq")
    last = rand_blocks[:, RAND - 1]
    owner = last // nblk
    offs = jnp.array(OFFSETS, jnp.int32)
    mine = owner[None, :] == (me + offs)[:, None]
    want = jnp.sum(jnp.where(mine, (last - owner * nblk)[None, :], 0), axis=1)
    req = jnp.broadcast_to(want[:, None, None], (NFAR, 8, 128)).astype(jnp.int32)
    dist = rand_blocks // nblk - me
    slot = jnp.where(dist < 0, dist + FAR, dist + FAR - 1)
    idx = jnp.where(dist == 0, rand_blocks - me * nblk + 1, nblk + 2 + slot)
    idx = idx.reshape(-1).astype(jnp.int32)

    cb = 256 if n <= 32 else 128
    rb = NG * width // (n * cb)
    ext = tok_dev + 2 * BLK + NFAR * BLK + NG
    dma = pltpu.SemaphoreType.DMA
    vm = pltpu.VMEM
    blocks = vm((ext // BLK, BLK, width), BF)
    square = vm((width, width), BF)
    piece = vm((n, rb, cb), BF)
    stat = vm((n, rb, 128), F32)
    scratch = [
        vm((ext, width), BF), square, square, square, square,
        vm((tok_dev, width), BF), blocks, blocks,
        vm((NG, width), BF), vm((tok_dev, width), BF), vm((NG, width), F32),
        vm((NFAR * BLK, tok_dev), BF), vm((NFAR * BLK, width), BF),
        vm((NFAR, 8, 128), jnp.int32),
        piece, piece, piece, piece, piece, stat, stat, piece,
        dma((5,)), dma((NFAR,)), dma((NFAR,)), dma((2 + NFAR,)), dma((2 + NFAR,)),
    ] + [dma(())] * 10
    anyspace = pl.BlockSpec(memory_space=pl.ANY)
    vmem = pl.BlockSpec(memory_space=pltpu.VMEM)
    return pl.pallas_call(
        functools.partial(mega, n),
        out_shape=jax.ShapeDtypeStruct((tok_dev, width), BF),
        in_specs=[anyspace] * 5 + [vmem] * 3 + [pl.BlockSpec(memory_space=pltpu.SMEM)],
        out_specs=vmem,
        scratch_shapes=scratch,
        compiler_params=pltpu.CompilerParams(
            collective_id=0, has_side_effects=True, vmem_limit_bytes=60 << 20
        ),
        name="sublayer",
    )(
        tokens, w_query, w_key, w_value, w_out, req,
        global_pos.reshape(NG, 1), global_pos.reshape(1, NG), idx,
    )


def solution(mesh):
    placed = (P("seq", None), P(), P(), P(), P(), P("seq", None), P())
    return jax.shard_map(
        functools.partial(body, mesh.shape["seq"]), mesh=mesh, in_specs=placed,
        out_specs=P("seq", None), check_vma=False,
    )
```

```python
import functools
import math

import jax
import jax.numpy as jnp
from jax import lax
from jax.experimental import pallas as pl
from jax.experimental.pallas import tpu as pltpu
from jax.sharding import PartitionSpec as P

HEADS = 16
HD = 64
BLK = 64
RAND = 3
NG = 128
FAR = 3
OFFSETS = tuple(range(-FAR, 0)) + tuple(range(1, FAR + 1))
NFAR = len(OFFSETS)
GH = 4
GL = GH * HD
EXP_SCALE = math.log2(math.e) / math.sqrt(HD)
SCORE_SCALE = 1.0 / math.sqrt(HD)
MESH = pl.DeviceIdType.MESH
BF = jnp.bfloat16
F32 = jnp.float32


def mega(
    n,
    tok_hbm, wq_hbm, wk_hbm, wv_hbm, wo_hbm, rbv_ref, grow_ref, rb_ref,
    out_ref,
    text, wq, wk, wv, wo, q, k, v, gq, sp, gf, sel, far,
    req_out, reqin, order, place, rs_out, rs_in, ag, cn_out, cn_in, cs_out, cs_in, ag2,
    load_sem, req_s, req_r, edge_s, edge_r,
    rs_s, rs_r, ag_s, ag_r, cn_s, cn_r, cs_s, cs_r, ag2_s, ag2_r,
):
    tok_dev, width = tok_hbm.shape
    nblk = tok_dev // BLK
    me = lax.axis_index("seq")
    _, rb, cb = ag.shape
    ncg = width // cb
    hpb = cb // HD
    groups = width // GL
    right0 = BLK + tok_dev
    far0 = right0 + BLK
    glob0 = far0 + NFAR * BLK

    own = text.at[pl.ds(BLK, tok_dev)]
    loads = [
        pltpu.make_async_copy(src, dst, load_sem.at[i])
        for i, (src, dst) in enumerate(
            ((tok_hbm, own), (wq_hbm, wq), (wk_hbm, wk), (wv_hbm, wv), (wo_hbm, wo))
        )
    ]
    for cp in loads:
        cp.start()

    text[0:BLK] = jnp.zeros((BLK, width), BF)
    text[right0:glob0] = jnp.zeros((glob0 - right0, width), BF)
    reqin[...] = jnp.zeros(reqin.shape, F32)
    base = rbv_ref[:, RAND - 1:RAND] - me * nblk
    for i, o in enumerate(OFFSETS):
        loc = base - o * nblk
        loc = jnp.where((loc >= 0) & (loc < nblk), loc, 0).astype(F32)
        req_out[i] = jnp.broadcast_to(jnp.sum(loc, axis=0, keepdims=True), (8, 128))

    barrier = pltpu.get_barrier_semaphore()

    def greet(o, c):
        pl.semaphore_signal(
            barrier, inc=1, device_id=(lax.rem(me + o, n),), device_id_type=MESH
        )
        return c

    lax.fori_loop(1, n, greet, 0)
    pl.semaphore_wait(barrier, n - 1)

    def to_all(src, dst, s_sem, r_sem):
        def one(o, c):
            peer = lax.rem(me + o, n)
            pltpu.make_async_remote_copy(
                src_ref=src(peer), dst_ref=dst.at[me], send_sem=s_sem, recv_sem=r_sem,
                device_id=(peer,), device_id_type=MESH,
            ).start()
            return c

        lax.fori_loop(1, n, one, 0)

    def wait_bytes(buf, sem):
        part = buf.at[pl.ds(0, n - 1)]
        pltpu.make_async_copy(part, part, sem).wait()

    def req_copy(i):
        return pltpu.make_async_remote_copy(
            src_ref=req_out.at[i], dst_ref=reqin.at[i], send_sem=req_s.at[i],
            recv_sem=req_r.at[i], device_id=(me + OFFSETS[i],), device_id_type=MESH,
        )

    def far_copy(i):
        return pltpu.make_async_remote_copy(
            src_ref=far.at[pl.ds(i * BLK, BLK)],
            dst_ref=text.at[pl.ds(far0 + i * BLK, BLK)],
            send_sem=edge_s.at[2 + i], recv_sem=edge_r.at[2 + i],
            device_id=(me - OFFSETS[i],), device_id_type=MESH,
        )

    def halo_copy(side):
        if side == 0:
            src, dst, dev = (BLK, right0, me - 1)
        else:
            src, dst, dev = (right0 - BLK, 0, me + 1)
        return pltpu.make_async_remote_copy(
            src_ref=text.at[pl.ds(src, BLK)], dst_ref=text.at[pl.ds(dst, BLK)],
            send_sem=edge_s.at[side], recv_sem=edge_r.at[side],
            device_id=(dev,), device_id_type=MESH,
        )

    def exists(o):
        return me + o >= 0 if o < 0 else me + o < n

    for i, o in enumerate(OFFSETS):
        @pl.when(exists(o))
        def _():
            req_copy(i).start()

    loads[0].wait()
    def project(src, s0, rows, w, dst, d0, step):
        def one(c, carry):
            a = pl.multiple_of(s0 + c * step, BLK)
            b = pl.multiple_of(d0 + c * step, BLK)
            val = jnp.dot(
                src[pl.ds(a, step)], w[...], preferred_element_type=F32
            ).astype(dst.dtype)
            if len(dst.shape) == 3:
                dst[pl.ds(d0 // BLK + c * (step // BLK), step // BLK)] = val.reshape(
                    step // BLK, BLK, width
                )
            else:
                dst[pl.ds(b, step)] = val
            return carry

        lax.fori_loop(0, rows // step, one, 0)

    diag = lax.broadcasted_iota(jnp.int32, (NG, NG), 0) == lax.broadcasted_iota(
        jnp.int32, (NG, NG), 1
    )
    gcol = jnp.sum(
        jnp.where(diag, (grow_ref[...] - me * tok_dev).astype(F32), 0.0), axis=1, keepdims=True
    )
    hit = gcol == lax.broadcasted_iota(jnp.int32, (NG, tok_dev), 1).astype(F32)
    sel[0:NG] = jnp.where(hit, 1.0, 0.0).astype(BF)
    project(sel, 0, NG, own, gf, 0, NG)
    for d in range(n):
        r, c = (d // ncg) * rb, (d % ncg) * cb
        rs_out[d] = gf[r:r + rb, c:c + cb].astype(BF)
    to_all(lambda p: rs_out.at[p], rs_in, rs_s, rs_r)

    lates = []
    for b in range(nblk):
        if b in (0, nblk - 1):
            lates.append(jnp.int32(1))
        else:
            r = rb_ref[b, RAND - 1] - me * nblk
            lates.append(jnp.where((r >= 0) & (r < nblk), 0, 1))
    early = nblk - sum(lates)
    seen = jnp.int32(0)
    spots = []
    for b in range(nblk):
        spots.append(jnp.where(lates[b] == 1, early + seen, b - seen))
        seen = seen + lates[b]
        place[b] = spots[b]
    for t in range(nblk):
        order[t] = sum(jnp.where(spots[b] == t, b, 0) for b in range(nblk))

    for i, o in enumerate(OFFSETS):
        @pl.when(exists(-o))
        def _():
            req_copy(i).wait_recv()
    col = lax.broadcasted_iota(jnp.int32, (BLK, tok_dev), 1)
    row = lax.broadcasted_iota(jnp.int32, (BLK, tok_dev), 0)
    away = (col - row).astype(F32)
    for i in range(NFAR):
        want = reqin[i, 0:1, 0:1] * BLK
        sel[i * BLK:(i + 1) * BLK] = jnp.where(away == want, 1.0, 0.0).astype(BF)
    project(sel, 0, NFAR * BLK, own, far, 0, 2 * BLK)

    loads[1].wait()
    project(text, BLK, tok_dev, wq, q, 0, 256)

    rs_in[me] = rs_out[me]
    wait_bytes(rs_in, rs_r)
    ag[me] = jnp.sum(rs_in[...].astype(F32), axis=0).astype(BF)
    to_all(lambda p: ag.at[me], ag, ag_s, ag_r)
    for side, o in ((0, -1), (1, 1)):
        @pl.when(exists(o))
        def _():
            halo_copy(side).start()
    for i, o in enumerate(OFFSETS):
        @pl.when(exists(-o))
        def _():
            far_copy(i).start()

    loads[2].wait()
    project(text, BLK, tok_dev, wk, k, BLK, 256)
    loads[3].wait()
    project(text, BLK, tok_dev, wv, v, BLK, 256)

    wait_bytes(ag, ag_r)
    for d in range(n):
        r, c = (d // ncg) * rb, (d % ncg) * cb
        gf[r:r + rb, c:c + cb] = ag[d].astype(F32)
    text[glob0:glob0 + NG] = gf[...].astype(BF)
    project(text, glob0, NG, wq, gq, 0, NG)

    lane = lax.broadcasted_iota(jnp.int32, (1, GL), 1) // HD
    masks = [jnp.where(lane == h, 1.0, 0.0).astype(BF) for h in range(GH)]
    lane_f = lax.broadcasted_iota(jnp.int32, (1, 128), 1)

    def stacked(x):
        return jnp.concatenate([x * m for m in masks], axis=0)

    def unstacked(x, rows):
        y = x[0:rows]
        for h in range(1, GH):
            y = jnp.where(lane == h, x[h * rows:(h + 1) * rows], y)
        return y

    NT = (((1,), (1,)), ((), ()))
    for g in range(groups):
        ls = slice(g * GL, (g + 1) * GL)
        s = lax.dot_general(
            stacked(gq[:, ls]), k[1:1 + nblk, :, ls].reshape(tok_dev, GL), NT, preferred_element_type=F32
        )
        m = jnp.max(s, axis=-1, keepdims=True)
        e = jnp.exp2((s - m) * EXP_SCALE)
        t = jnp.sum(e, axis=-1, keepdims=True)
        num = unstacked(
            jnp.dot(e.astype(BF), v[1:1 + nblk, :, ls].reshape(tok_dev, GL), preferred_element_type=F32), NG
        )
        m = m * SCORE_SCALE
        for part in range(GL // cb):
            stat = jnp.zeros((NG, 128), F32)
            for j in range(hpb):
                h = part * hpb + j
                stat = jnp.where(lane_f == j, m[h * NG:(h + 1) * NG], stat)
                stat = jnp.where(lane_f == hpb + j, t[h * NG:(h + 1) * NG], stat)
            cg = g * (GL // cb) + part
            for rg in range(NG // rb):
                d = rg * ncg + cg
                cn_out[d] = num[rg * rb:(rg + 1) * rb, part * cb:(part + 1) * cb].astype(BF)
                cs_out[d] = stat[rg * rb:(rg + 1) * rb]
    to_all(lambda p: cs_out.at[p], cs_in, cs_s, cs_r)
    to_all(lambda p: cn_out.at[p], cn_in, cn_s, cn_r)

    for w, dst in ((wk, k), (wv, v)):
        project(text, glob0, NG, w, dst, glob0, NG)

    keys_all = (3 + RAND) * BLK + NG
    key_col = lax.broadcasted_iota(jnp.int32, (1, keys_all), 1)

    def attend(late, t, carry):
        b = order[t]
        picks = []
        for r in range(RAND):
            rel = rb_ref[b, r] - me * nblk
            dev = lax.div(rel + FAR * nblk, nblk)
            slot = jnp.where(dev < FAR, dev, dev - 1)
            pick = jnp.where(dev == FAR, rel + 1, nblk + 2 + slot)
            picks.append(jnp.minimum(jnp.maximum(pick, 0), nblk + 1 + NFAR))
        if late:
            lead = jnp.where((me == 0) & (b == 0), BLK, 0)
            tail = jnp.where((me == n - 1) & (b == nblk - 1), 2 * BLK, 3 * BLK)
            bad = (key_col < lead) | ((key_col >= tail) & (key_col < 3 * BLK))
            bias = jnp.where(bad, -1e30, 0.0)

        def rows(ref, ls):
            return jnp.concatenate(
                [ref[b + i, :, ls] for i in range(3)]
                + [ref[i, :, ls] for i in picks]
                + [ref[glob0 // BLK:, :, ls].reshape(NG, GL)],
                axis=0,
            )

        for g in range(groups):
            ls = slice(g * GL, (g + 1) * GL)
            s = lax.dot_general(
                stacked(q[b, :, ls]), rows(k, ls), NT, preferred_element_type=F32
            )
            if late:
                s = s + bias
            m = jnp.max(s, axis=-1, keepdims=True)
            e = jnp.exp2((s - m) * EXP_SCALE)
            inv = 1.0 / jnp.sum(e, axis=-1, keepdims=True)
            o = jnp.dot((e * inv).astype(BF), rows(v, ls), preferred_element_type=F32)
            sp[t, :, ls] = unstacked(o, BLK).astype(BF)
        return carry

    lax.fori_loop(0, nblk // 2, functools.partial(attend, False), 0)

    cs_in[me] = cs_out[me]
    cn_in[me] = cn_out[me]
    wait_bytes(cs_in, cs_r)
    wait_bytes(cn_in, cn_r)
    peak = jnp.max(cs_in[...], axis=0)
    lane_c = lax.broadcasted_iota(jnp.int32, (1, cb), 1) // HD

    def spread(x, first):
        y = jnp.broadcast_to(x[:, first:first + 1], (rb, cb))
        for j in range(1, hpb):
            y = jnp.where(lane_c == j, x[:, first + j:first + j + 1], y)
        return y

    def merge(s, c):
        num, den = c
        stat = cs_in[s]
        fac = spread(jnp.exp(stat - peak), 0)
        return num + cn_in[s].astype(F32) * fac, den + spread(stat, hpb) * fac

    zero = jnp.zeros((rb, cb), F32)
    num, den = lax.fori_loop(0, n, merge, (zero, zero))
    ag2[me] = (num / den).astype(BF)
    to_all(lambda p: ag2.at[me], ag2, ag2_s, ag2_r)

    for side, o in ((0, 1), (1, -1)):
        @pl.when(exists(o))
        def _():
            halo_copy(side).wait_recv()
    for i, o in enumerate(OFFSETS):
        @pl.when(exists(o))
        def _():
            far_copy(i).wait_recv()
    for w, dst in ((wk, k), (wv, v)):
        project(text, 0, BLK, w, dst, 0, BLK)
        project(text, right0, BLK, w, dst, right0, BLK)
        project(text, far0, NFAR * BLK, w, dst, far0, 128)

    lax.fori_loop(nblk // 2, nblk, functools.partial(attend, True), 0)

    wait_bytes(ag2, ag2_r)
    for d in range(n):
        r, c = (d // ncg) * rb, (d % ncg) * cb
        gf[r:r + rb, c:c + cb] = ag2[d].astype(F32)
    gq[...] = gf[...].astype(BF)
    loads[4].wait()
    step = 256

    def finish(c, carry):
        at = pl.multiple_of(c * step, step)
        pos = me * tok_dev + at + lax.broadcasted_iota(jnp.int32, (step, NG), 0)
        one = jnp.where(pos == grow_ref[...], 1.0, 0.0)
        is_g = jnp.max(one, axis=-1, keepdims=True) > 0.5
        put = jnp.dot(one.astype(BF), gq[...], preferred_element_type=F32)
        own_rows = jnp.concatenate(
            [sp[place[c * (step // BLK) + i]] for i in range(step // BLK)], axis=0
        )
        att = jnp.where(is_g, put, own_rows.astype(F32)).astype(BF)
        out_ref[pl.ds(at, step)] = jnp.dot(
            att, wo[...], preferred_element_type=F32
        ).astype(BF)
        return carry

    lax.fori_loop(0, tok_dev // step, finish, 0)

    for i, o in enumerate(OFFSETS):
        @pl.when(exists(o))
        def _():
            req_copy(i).wait_send()

        @pl.when(exists(-o))
        def _():
            far_copy(i).wait_send()
    for side, o in ((0, -1), (1, 1)):
        @pl.when(exists(o))
        def _():
            halo_copy(side).wait_send()
    for buf, sem in ((rs_out, rs_s), (ag, ag_s), (cn_out, cn_s), (cs_out, cs_s), (ag2, ag2_s)):
        wait_bytes(buf, sem)


def body(n, tokens, w_query, w_key, w_value, w_out, rand_blocks, global_pos):
    tok_dev, width = tokens.shape
    nblk = tok_dev // BLK
    cb = 256 if n <= 32 else 128
    rb = NG * width // (n * cb)
    ext = tok_dev + 2 * BLK + NFAR * BLK + NG
    dma = pltpu.SemaphoreType.DMA
    vm = pltpu.VMEM
    blocks = vm((ext // BLK, BLK, width), BF)
    own_blocks = vm((nblk, BLK, width), BF)
    square = vm((width, width), BF)
    piece = vm((n, rb, cb), BF)
    stat = vm((n, rb, 128), F32)
    scratch = [
        vm((ext, width), BF), square, square, square, square,
        own_blocks, blocks, blocks,
        vm((NG, width), BF), own_blocks, vm((NG, width), F32),
        vm((NFAR * BLK, tok_dev), BF), vm((NFAR * BLK, width), BF),
        vm((NFAR, 8, 128), F32), vm((NFAR, 8, 128), F32),
        pltpu.SMEM((nblk,), jnp.int32), pltpu.SMEM((nblk,), jnp.int32),
        piece, piece, piece, piece, piece, stat, stat, piece,
        dma((5,)), dma((NFAR,)), dma((NFAR,)), dma((2 + NFAR,)), dma((2 + NFAR,)),
    ] + [dma(())] * 10
    anyspace = pl.BlockSpec(memory_space=pl.ANY)
    vmem = pl.BlockSpec(memory_space=pltpu.VMEM)
    return pl.pallas_call(
        functools.partial(mega, n),
        out_shape=jax.ShapeDtypeStruct((tok_dev, width), BF),
        in_specs=[anyspace] * 5 + [vmem] * 2 + [pl.BlockSpec(memory_space=pltpu.SMEM)],
        out_specs=vmem,
        scratch_shapes=scratch,
        compiler_params=pltpu.CompilerParams(
            collective_id=0, has_side_effects=True, vmem_limit_bytes=60 << 20
        ),
        name="sublayer",
    )(
        tokens, w_query, w_key, w_value, w_out, rand_blocks,
        global_pos.reshape(1, NG), rand_blocks,
    )


def solution(mesh):
    placed = (P("seq", None), P(), P(), P(), P(), P("seq", None), P())
    return jax.shard_map(
        functools.partial(body, mesh.shape["seq"]), mesh=mesh, in_specs=placed,
        out_specs=P("seq", None), check_vma=False,
    )
```
